32 devices in a mesh: rows: 16 (over z, x, core), cols: 2 (over y).
Axes of the slice: x: 2, y: 2, z: 4, core: 2. Of those that a mesh axis runs over, the one named last changes fastest.
Arguments:
- cell_cost: float32 [128, 1024], P('rows', 'cols'), may hold values from 0.2 to 8, as said below
- blocked: int32 [128, 1024], P('rows', 'cols'), may hold values 0 or 1
- move_table: int32 [8, 8], replicated, may hold values from 0 to 7
- anchor_cells: int32 [16, 2, 128], P('rows', 'cols'), may hold values from 0 to 4095
- anchor_mass: float32 [16, 2, 128], P('rows', 'cols'), may hold values from 0.5 to 2
Outputs:
- values: float32 [8, 128, 1024], P(None, 'rows', 'cols')
- visits: float32 [128, 1024], P('rows', 'cols')
The draws below stay inside these ranges and needn't reach their ends.
Inputs may be any that keep to these rules, and one draw needn't show every extreme that they name: `cell_cost`: positive costs. `anchor_cells`: row-major cell index within the device's own tile.
All inputs are finite; a program needn't handle non-finite values. No bound on the sum of `blocked` on one device may be relied on, other than what follows from the above.
Results may differ from the reference program's by a relative error of at most 0.0003.
Values sent between devices are 32-bit elements; how exact they have to be, the bound alone decides.
A program may use at most 64 MiB of HBM per device.

```python
import math
import jax
import jax.numpy as jnp
from jax import lax

TR = 8
TC = 512
ITERS = 20
HEADINGS = 8
ANCHORS = 128
NR = 128
NC = 1024
N_ROWS = 16
N_COLS = 2


def draw_cell_cost(key, part):
    spread = jax.random.uniform(key, (NR, NC), jnp.float32, jnp.log(0.2), jnp.log(8.0))
    return jnp.exp(spread)


def plant(drawn, rng, smallest, high):
    place = [jax.random.randint(jax.random.fold_in(rng, axis), (), 0, length) for axis, length in enumerate(drawn.shape)]
    longest = drawn.shape.index(max(drawn.shape))
    neighbour = place[:longest] + [(place[longest] + 1) % drawn.shape[longest]] + place[longest + 1:]
    return drawn.at[tuple(place)].set(smallest).at[tuple(neighbour)].set(high)


def steps_of(key, dims, split, smallest, high):
    def one(axis_at, shards_of):
        steps = jax.random.uniform(jax.random.fold_in(jax.random.fold_in(key, 6), axis_at), (shards_of,), jnp.float32, smallest / len(split), high / len(split))
        return jnp.repeat(jnp.exp(steps), dims[axis_at] // shards_of).reshape((-1,) + (1,) * (len(dims) - axis_at - 1))

    factor_of = one(*split[0])
    for cut in split[1:]:
        factor_of = factor_of * one(*cut)
    return factor_of


def setup_inputs(seed: int = 0) -> dict:
    keys = jax.random.split(jax.random.key(seed), 6)
    cell_cost = draw_cell_cost(jax.random.fold_in(keys[5], 71), 0)
    blocked = plant((jax.random.randint(keys[1], (NR, NC), 0, 20) < 3).astype(jnp.int32), jax.random.fold_in(keys[1], 1), 0, 1)
    move_table = plant(jax.random.randint(keys[2], (HEADINGS, HEADINGS), 0, 8), jax.random.fold_in(keys[2], 1), 0, 7).astype(jnp.int32)
    anchor_cells = plant(jax.random.randint(keys[3], (N_ROWS, N_COLS, ANCHORS), 0, TR * TC), jax.random.fold_in(keys[3], 1), 0, (TR * TC) - 1).astype(jnp.int32)
    anchor_mass = jnp.clip(jnp.exp(math.log(2.0) - 1.3862944 * jax.random.uniform(keys[4], (N_ROWS, N_COLS, ANCHORS), jnp.float32) ** steps_of(keys[4], (N_ROWS, N_COLS, ANCHORS), ((0, 16), (1, 2)), -0.2, 0.2)), 0.5, 2.0)
    return {"cell_cost": cell_cost, "blocked": blocked, "move_table": move_table, "anchor_cells": anchor_cells, "anchor_mass": anchor_mass}


PENALTY = 3.0
ROW_STEP = (0, -1, -1, -1, 0, 1, 1, 1)
COL_STEP = (1, 1, 0, -1, -1, -1, 0, 1)


def successors(value, penalty_pad):
    total_rows = value.shape[1]
    total_cols = value.shape[2]
    padded = jnp.pad(value, ((0, 0), (1, 1), (1, 1)))
    parts = []
    for heading in range(8):
        top = 1 + ROW_STEP[heading]
        left = 1 + COL_STEP[heading]
        parts.append(padded[heading, top:top + total_rows, left:left + total_cols]
                     + penalty_pad[top:top + total_rows, left:left + total_cols])
    return jnp.stack(parts)


def log_total(chosen):
    largest = jnp.max(chosen, axis=0)
    return largest + jnp.log(jnp.sum(jnp.exp(chosen - largest[None]), axis=0))


def reference(cell_cost, blocked, move_table, anchor_cells, anchor_mass):
    total_rows, total_cols = cell_cost.shape
    penalty = -PENALTY * blocked.astype(jnp.float32)
    penalty_pad = jnp.pad(penalty, 1)
    value = jnp.zeros((8, total_rows, total_cols), jnp.float32)
    stored = []
    for turn in range(ITERS):
        stored.append(value)
        shifted = successors(value, penalty_pad)
        totals = lax.map(lambda heading_row: log_total(jnp.take(shifted, heading_row, axis=0)), move_table)
        value = totals - cell_cost[None]
    values = value / ITERS

    tile_rows = jnp.arange(N_ROWS, dtype=jnp.int32)[:, None, None] * TR + anchor_cells // TC
    tile_cols = jnp.arange(N_COLS, dtype=jnp.int32)[None, :, None] * TC + anchor_cells % TC
    start = jnp.zeros((total_rows, total_cols), jnp.float32)
    start = start.at[tile_rows.reshape(-1), tile_cols.reshape(-1)].add(anchor_mass.reshape(-1))
    density = jnp.broadcast_to(start[None] / 8.0, (8, total_rows, total_cols))
    visits = jnp.zeros((total_rows, total_cols), jnp.float32)
    headings = jnp.arange(8, dtype=jnp.int32)
    for turn in range(ITERS):
        shifted = successors(stored[ITERS - 1 - turn], penalty_pad)

        def add_heading(arrivals, inputs):
            heading_row, mass = inputs
            chosen = jnp.take(shifted, heading_row, axis=0)
            policy = jnp.exp(chosen - log_total(chosen)[None])
            selector = (heading_row[None, :] == headings[:, None]).astype(jnp.float32)
            flow = mass[None] * policy
            arrivals = arrivals + jnp.einsum('ka,axy->kxy', selector, flow, precision=lax.Precision.HIGHEST)
            return arrivals, None

        arrivals, unused = lax.scan(add_heading, jnp.zeros((8, total_rows, total_cols), jnp.float32), (move_table, density))
        padded = jnp.pad(arrivals, ((0, 0), (1, 1), (1, 1)))
        parts = []
        for heading in range(8):
            top = 1 - ROW_STEP[heading]
            left = 1 - COL_STEP[heading]
            parts.append(padded[heading, top:top + total_rows, left:left + total_cols])
        density = jnp.stack(parts)
        visits = visits + jnp.sum(density, axis=0)
    return values, visits
```

```python
import functools
import math

import jax
import jax.numpy as jnp
from jax import lax
from jax.experimental import pallas as pl
from jax.experimental.pallas import tpu as pltpu
from jax.sharding import PartitionSpec as P

ITERS = 20
PENALTY = 3.0
ROW_STEP = (0, -1, -1, -1, 0, 1, 1, 1)
COL_STEP = (1, 1, 0, -1, -1, -1, 0, 1)
MESH = pl.DeviceIdType.MESH
LANES = 128
LOG2E = math.log2(math.e)
SMALLEST = 2.0**-60
CHUNK = 32
PAD = 8


def prepare(cost_ref, blocked_ref, cells_ref, mass_ref, out_ref):
    height, width = cost_ref.shape
    entries = cells_ref.shape[-1]
    cells = cells_ref[...].reshape(1, entries)
    masses = mass_ref[...].reshape(1, entries) * 0.125
    row = jnp.zeros((1, entries), jnp.int32)
    for i in range(1, height):
        row = row + (cells >= i * width).astype(jnp.int32)
    col = cells - row * width
    rows = lax.broadcasted_iota(jnp.int32, (height, entries), 0)
    cols = lax.broadcasted_iota(jnp.int32, (width, entries), 0)
    at_row = jnp.where(rows == row, masses, 0.0)
    at_col = (cols == col).astype(jnp.float32)
    out_ref[0] = cost_ref[...] * LOG2E
    out_ref[1] = blocked_ref[...].astype(jnp.float32) * (-PENALTY * LOG2E)
    out_ref[2] = lax.dot_general(
        at_row,
        at_col,
        (((1,), (1,)), ((), ())),
        precision=lax.Precision.HIGHEST,
        preferred_element_type=jnp.float32,
    )


def gather(n_rows, n_cols, strip, halo, x_ref, buf_ref, send_sem, recv_sem):
    me_r = lax.axis_index("rows")
    me_c = lax.axis_index("cols")
    blocks = x_ref.shape[-1] // LANES
    strips = n_rows * n_cols
    per = 2 * LANES // strip
    for q in range(blocks):
        block = me_c * blocks + q
        first = (block * LANES + halo + strip - 1) // strip - LANES // strip
        for j in range(per):
            s = first + j
            half = 1 if j < per // 2 else 0
            ok = jnp.logical_and(s >= 0, s < strips)
            s = jnp.clip(s, 0, strips - 1)
            to_c = s // n_rows
            to_r = s - to_c * n_rows
            mine = jnp.logical_and(to_c == me_c, to_r == me_r)
            src = x_ref.at[:, :, q * LANES : (q + 1) * LANES]
            dst = buf_ref.at[half, me_r]

            @pl.when(jnp.logical_and(ok, jnp.logical_not(mine)))
            def _():
                pltpu.make_async_remote_copy(
                    src_ref=src,
                    dst_ref=dst,
                    send_sem=send_sem.at[q * per + j],
                    recv_sem=recv_sem.at[half, me_r],
                    device_id=(to_r, to_c),
                    device_id_type=MESH,
                ).start()

            @pl.when(jnp.logical_and(ok, mine))
            def _():
                pltpu.make_async_copy(src, dst, recv_sem.at[half, me_r]).start()

    s = me_c * n_rows + me_r
    low = (s * strip - halo + LANES) // LANES - 1
    for half in range(2):
        b = low + half

        @pl.when(jnp.logical_and(b >= 0, b < blocks * n_cols))
        def _():
            def one(r, carry):
                ref = buf_ref.at[half, r]
                pltpu.make_async_copy(ref, ref, recv_sem.at[half, r]).wait()
                return carry

            lax.fori_loop(0, n_rows, one, 0)

    for q in range(blocks):
        block = me_c * blocks + q
        first = (block * LANES + halo + strip - 1) // strip - LANES // strip
        for j in range(per):
            s = first + j
            ok = jnp.logical_and(s >= 0, s < strips)
            s = jnp.clip(s, 0, strips - 1)
            to_c = s // n_rows
            to_r = s - to_c * n_rows
            mine = jnp.logical_and(to_c == me_c, to_r == me_r)
            src = x_ref.at[:, :, q * LANES : (q + 1) * LANES]

            @pl.when(jnp.logical_and(ok, jnp.logical_not(mine)))
            def _():
                pltpu.make_async_copy(src, src, send_sem.at[q * per + j]).wait()


def sweep(
    n_rows, n_cols, strip, halo, where_ref, table_ref, count_ref, buf_ref, out_ref,
    vst, est, rst, gbuf, cost, pen, start, visits, splat, bad,
):
    total = cost.shape[0]
    s = where_ref[0]
    begin = s * strip - halo
    shift = where_ref[1]
    lane = lax.broadcasted_iota(jnp.int32, (8, LANES), 1)
    col = lane + begin
    inside8 = jnp.logical_and(col >= 0, col < n_rows * n_cols * strip)
    zero8 = jnp.zeros((8, LANES), jnp.float32)

    for g in range(2):
        for k in range(8):
            vst[g, k, 0:PAD, :] = zero8
            vst[g, k, PAD + total : PAD + total + PAD, :] = zero8
            gbuf[g, k, 0:PAD, :] = zero8
            gbuf[g, k, PAD + total : PAD + total + PAD, :] = zero8
    pen[0:PAD, :] = zero8
    pen[PAD + total : PAD + total + PAD, :] = zero8
    bad[...] = zero8
    for h in range(8):
        for k in range(8):
            splat[h * 8 + k] = jnp.full((8, LANES), count_ref[h, k], jnp.float32)
    back = lax.rem(LANES - shift, LANES)
    for r in range(n_rows):
        rows = slice(r * 8, r * 8 + 8)

        def region(i):
            a = pltpu.roll(buf_ref[0, r, i], back, 1)
            b = pltpu.roll(buf_ref[1, r, i], back, 1)
            return jnp.where(inside8, jnp.where(lane < LANES - shift, a, b), 0.0)

        cost[rows, :] = region(0)
        pen[PAD + r * 8 : PAD + r * 8 + 8, :] = region(1)
        start[rows, :] = region(2)

    inside = jnp.broadcast_to(inside8[None], (CHUNK // 8, 8, LANES)).reshape(CHUNK, LANES)
    chunks = [c * CHUNK for c in range(total // CHUNK)]

    def run(direct):
        for k in range(8):
            for r0 in chunks:
                vst[0, k, PAD + r0 : PAD + r0 + CHUNK, :] = jnp.zeros((CHUNK, LANES), jnp.float32)

        def back_step(n, carry):
            now = lax.rem(n, 2)
            for r0 in chunks:
                rows = slice(r0, r0 + CHUNK)
                shifted = []
                for k in range(8):
                    at = slice(PAD + r0 + ROW_STEP[k], PAD + r0 + ROW_STEP[k] + CHUNK)
                    value = vst[now, k, at, :] + pen[at, :]
                    if COL_STEP[k]:
                        value = pltpu.roll(value, (-COL_STEP[k]) % LANES, 1)
                    shifted.append(value)
                if not direct:
                    largest = functools.reduce(jnp.maximum, shifted)
                    for k in range(8):
                        est[n, k, rows, :] = jnp.exp2(shifted[k] - largest)
                else:
                    for k in range(8):
                        est[n, k, rows, :] = shifted[k]
                smallest = None
                for h in range(8):
                    chosen = [est[n, table_ref[h, a], rows, :] for a in range(8)]
                    if direct:
                        largest = functools.reduce(jnp.maximum, chosen)
                        chosen = [jnp.exp2(q - largest) for q in chosen]
                    while len(chosen) > 1:
                        chosen = [chosen[i] + chosen[i + 1] for i in range(0, len(chosen), 2)]
                    sums = chosen[0]
                    level = jnp.log2(sums) + largest
                    rst[n, h, rows, :] = level if direct else 1.0 / sums
                    vst[1 - now, h, PAD + r0 : PAD + r0 + CHUNK, :] = jnp.where(
                        inside, level - cost[rows, :], 0.0
                    )
                    smallest = sums if h == 0 else jnp.minimum(smallest, sums)
                if not direct:
                    for i in range(CHUNK // 8):
                        ok = smallest[i * 8 : i * 8 + 8] >= SMALLEST
                        bad[...] = jnp.where(ok, bad[...], 1.0)
            return carry

        lax.fori_loop(0, ITERS, back_step, 0)

        def flow(n, slot, r0, density):
            rows = slice(r0, r0 + CHUNK)
            at = slice(PAD + r0, PAD + r0 + CHUNK)

            def weight(h, k):
                one = splat[h * 8 + k]
                return jnp.broadcast_to(one[None], (CHUNK // 8, 8, LANES)).reshape(CHUNK, LANES)

            if not direct:
                scaled = [density[h] * rst[n, h, rows, :] for h in range(8)]
                for k in range(8):
                    mass = functools.reduce(
                        jnp.add, [weight(h, k) * scaled[h] for h in range(8)]
                    )
                    gbuf[slot, k, at, :] = mass * est[n, k, rows, :]
            else:
                for k in range(8):
                    here = est[n, k, rows, :]
                    mass = jnp.zeros((CHUNK, LANES), jnp.float32)
                    for h in range(8):
                        policy = jnp.exp2(jnp.minimum(here - rst[n, h, rows, :], 0.0))
                        mass = mass + weight(h, k) * (density[h] * policy)
                    gbuf[slot, k, at, :] = mass

        def arrive(slot, r0):
            density = []
            for k in range(8):
                at = slice(PAD + r0 - ROW_STEP[k], PAD + r0 - ROW_STEP[k] + CHUNK)
                mass = gbuf[slot, k, at, :]
                if COL_STEP[k]:
                    mass = pltpu.roll(mass, COL_STEP[k] % LANES, 1)
                density.append(jnp.where(inside, mass, 0.0))
            return density

        for r0 in chunks:
            first = start[r0 : r0 + CHUNK, :]
            flow(ITERS - 1, 0, r0, [first] * 8)
            visits[r0 : r0 + CHUNK, :] = jnp.zeros((CHUNK, LANES), jnp.float32)

        def forward_step(t, carry):
            slot = lax.rem(t + 1, 2)
            for r0 in chunks:
                rows = slice(r0, r0 + CHUNK)
                density = arrive(slot, r0)
                visits[rows, :] = visits[rows, :] + functools.reduce(jnp.add, density)
                flow(ITERS - 1 - t, 1 - slot, r0, density)
            return carry

        lax.fori_loop(1, ITERS, forward_step, 0)
        for r0 in chunks:
            rows = slice(r0, r0 + CHUNK)
            density = arrive((ITERS - 1) % 2, r0)
            visits[rows, :] = visits[rows, :] + functools.reduce(jnp.add, density)

    run(False)
    pl.when(jnp.max(bad[...]) > 0.0)(lambda: run(True))

    group = LANES // strip
    packs = out_ref.shape[1] - 1
    scale = 1.0 / (LOG2E * ITERS)
    for r in range(n_rows):
        at = slice(PAD + r * 8, PAD + r * 8 + 8)
        for p in range(packs):
            packed = zero8
            for g in range(min(group, 8)):
                value = pltpu.roll(vst[ITERS % 2, p * group + g, at, :], (g * strip - halo) % LANES, 1)
                low = g * strip
                keep = jnp.logical_and(lane >= low, lane < low + strip)
                packed = jnp.where(keep, value, packed)
            out_ref[r, p] = packed * scale
        out_ref[r, packs] = pltpu.roll(visits[r * 8 : r * 8 + 8, :], (-halo) % LANES, 1)


def scatter(n_rows, strip, x_ref, values_ref, visits_ref, recv, send_sem, recv_sem):
    me_r = lax.axis_index("rows")
    me_c = lax.axis_index("cols")
    local = pltpu.make_async_copy(x_ref.at[me_r], recv.at[me_r], recv_sem.at[me_r])
    local.start()

    def partner(d):
        return lax.rem(me_r + d, n_rows)

    def send(d, carry):
        to = partner(d)
        pltpu.make_async_remote_copy(
            src_ref=x_ref.at[to],
            dst_ref=recv.at[me_r],
            send_sem=send_sem.at[to],
            recv_sem=recv_sem.at[me_r],
            device_id=(to, me_c),
            device_id_type=MESH,
        ).start()
        return carry

    lax.fori_loop(1, n_rows, send, 0)

    def arrived(r, carry):
        pltpu.make_async_copy(recv.at[r], recv.at[r], recv_sem.at[r]).wait()
        return carry

    lax.fori_loop(0, n_rows, arrived, 0)
    group = LANES // strip
    packs = x_ref.shape[1] - 1
    lane = lax.broadcasted_iota(jnp.int32, (8, LANES), 1)
    width = visits_ref.shape[-1]
    for q in range(width // LANES):
        cols = slice(q * LANES, (q + 1) * LANES)

        def assemble(pack, source):
            whole = None
            for i in range(group):
                piece = recv[q * group + i, pack]
                move = (i * strip - source) % LANES
                if move:
                    piece = pltpu.roll(piece, move, 1)
                whole = piece if i == 0 else jnp.where(lane >= i * strip, piece, whole)
            return whole

        for h in range(8):
            values_ref[h, :, cols] = assemble(h // group, (h % group) * strip)
        visits_ref[:, cols] = assemble(packs, 0)

    def sent(d, carry):
        to = partner(d)
        pltpu.make_async_copy(x_ref.at[to], x_ref.at[to], send_sem.at[to]).wait()
        return carry

    lax.fori_loop(1, n_rows, sent, 0)


def on_device(n_rows, n_cols, cell_cost, blocked, move_table, anchor_cells, anchor_mass):
    height, width = cell_cost.shape
    strip = width // n_rows
    halo = (LANES - strip) // 2
    assert height == 8 and strip * n_rows == width and halo >= 2 * ITERS
    total = height * n_rows
    group = LANES // strip
    packs = -(-8 // group)
    vmem = pl.BlockSpec(memory_space=pltpu.VMEM)
    smem = pl.BlockSpec(memory_space=pltpu.SMEM)
    f32 = jnp.float32

    tile = pl.pallas_call(
        prepare,
        out_shape=jax.ShapeDtypeStruct((3, height, width), f32),
        in_specs=[vmem] * 4,
        out_specs=vmem,
        name="prepare",
    )(cell_cost, blocked, anchor_cells, anchor_mass)

    sends = (width // LANES) * (2 * LANES // strip)
    buf = pl.pallas_call(
        functools.partial(gather, n_rows, n_cols, strip, halo),
        out_shape=jax.ShapeDtypeStruct((2, n_rows, 3, height, LANES), f32),
        in_specs=[vmem],
        out_specs=vmem,
        scratch_shapes=[
            pltpu.SemaphoreType.DMA((sends,)),
            pltpu.SemaphoreType.DMA((2, n_rows)),
        ],
        compiler_params=pltpu.CompilerParams(has_side_effects=True),
        name="gather",
    )(tile)

    index = lax.axis_index("cols") * n_rows + lax.axis_index("rows")
    begin = index * strip - halo
    where = jnp.stack([index, (begin + LANES) % LANES]).astype(jnp.int32)
    headings = jnp.arange(8, dtype=jnp.int32)
    counts = jnp.sum((move_table[:, None, :] == headings[None, :, None]).astype(f32), axis=-1)

    padded = total + 2 * PAD
    packed = pl.pallas_call(
        functools.partial(sweep, n_rows, n_cols, strip, halo),
        out_shape=jax.ShapeDtypeStruct((n_rows, packs + 1, height, LANES), f32),
        in_specs=[smem, smem, smem, vmem],
        out_specs=vmem,
        scratch_shapes=[
            pltpu.VMEM((2, 8, padded, LANES), f32),
            pltpu.VMEM((ITERS, 8, total, LANES), f32),
            pltpu.VMEM((ITERS, 8, total, LANES), f32),
            pltpu.VMEM((2, 8, padded, LANES), f32),
            pltpu.VMEM((total, LANES), f32),
            pltpu.VMEM((padded, LANES), f32),
            pltpu.VMEM((total, LANES), f32),
            pltpu.VMEM((total, LANES), f32),
            pltpu.VMEM((64, 8, LANES), f32),
            pltpu.VMEM((8, LANES), f32),
        ],
        compiler_params=pltpu.CompilerParams(vmem_limit_bytes=67043328),
        name="sweep",
    )(where, move_table, counts, buf)

    return pl.pallas_call(
        functools.partial(scatter, n_rows, strip),
        out_shape=(
            jax.ShapeDtypeStruct((8, height, width), f32),
            jax.ShapeDtypeStruct((height, width), f32),
        ),
        in_specs=[vmem],
        out_specs=(vmem, vmem),
        scratch_shapes=[
            pltpu.VMEM((n_rows, packs + 1, height, LANES), f32),
            pltpu.SemaphoreType.DMA((n_rows,)),
            pltpu.SemaphoreType.DMA((n_rows,)),
        ],
        compiler_params=pltpu.CompilerParams(has_side_effects=True),
        name="scatter",
    )(packed)


def solution(mesh):
    placed = (
        P("rows", "cols"),
        P("rows", "cols"),
        P(),
        P("rows", "cols", None),
        P("rows", "cols", None),
    )
    return jax.shard_map(
        functools.partial(on_device, mesh.shape["rows"], mesh.shape["cols"]),
        mesh=mesh,
        in_specs=placed,
        out_specs=(P(None, "rows", "cols"), P("rows", "cols")),
        check_vma=False,
    )
```

```python
import functools
import math

import jax
import jax.numpy as jnp
from jax import lax
from jax.experimental import pallas as pl
from jax.experimental.pallas import tpu as pltpu
from jax.sharding import PartitionSpec as P

ITERS = 20
PENALTY = 3.0
ROW_STEP = (0, -1, -1, -1, 0, 1, 1, 1)
COL_STEP = (1, 1, 0, -1, -1, -1, 0, 1)
MESH = pl.DeviceIdType.MESH
LANES = 128
LOG2E = math.log2(math.e)
SMALLEST = 2.0**-60
CHUNK = 32
PAD = 8


def prepare(n_rows, strip, halo, cost_ref, blocked_ref, table_ref, cells_ref, mass_ref, out_ref, count_ref):
    height, width = cost_ref.shape
    entries = cells_ref.shape[-1]
    cells = cells_ref[...].reshape(1, entries)
    masses = mass_ref[...].reshape(1, entries) * 0.125
    row = jnp.zeros((1, entries), jnp.int32)
    for i in range(1, height):
        row = row + (cells >= i * width).astype(jnp.int32)
    col = cells - row * width
    rows = lax.broadcasted_iota(jnp.int32, (height, entries), 0)
    cols = lax.broadcasted_iota(jnp.int32, (width, entries), 0)
    at_row = jnp.where(rows == row, masses, 0.0)
    at_col = (cols == col).astype(jnp.float32)
    start = lax.dot_general(
        at_row,
        at_col,
        (((1,), (1,)), ((), ())),
        precision=lax.Precision.HIGHEST,
        preferred_element_type=jnp.float32,
    )
    fields = (
        cost_ref[...] * LOG2E,
        blocked_ref[...].astype(jnp.float32) * (-PENALTY * LOG2E),
        start,
    )
    lane = lax.broadcasted_iota(jnp.int32, (height, LANES), 1)
    zero = jnp.zeros((height, LANES), jnp.float32)
    edge = -(-halo // strip)
    for slot, place in enumerate([*range(n_rows), *range(-edge, 0), *range(n_rows, n_rows + edge)]):
        begin = place * strip - halo
        block, off = begin // LANES, begin % LANES
        for f, field in enumerate(fields):

            def part(b):
                if b < 0 or b >= width // LANES:
                    return zero
                piece = field[:, b * LANES : (b + 1) * LANES]
                return pltpu.roll(piece, LANES - off, 1) if off else piece

            out_ref[slot, f] = jnp.where(lane < LANES - off, part(block), part(block + 1))

    table = table_ref[...]
    heading = lax.broadcasted_iota(jnp.int32, table.shape, 1)
    counts = jnp.zeros(table.shape, jnp.float32)
    for k in range(8):
        times = jnp.sum((table == k).astype(jnp.float32), axis=1, keepdims=True)
        counts = jnp.where(heading == k, times, counts)
    count_ref[...] = counts


def gather(n_rows, n_cols, edge, x_ref, buf_ref, send_sem, recv_sem):
    me_r = lax.axis_index("rows")
    me_c = lax.axis_index("cols")
    has_left = me_c > 0
    has_right = me_c < n_cols - 1
    left = jnp.maximum(me_c - 1, 0)
    right = jnp.minimum(me_c + 1, n_cols - 1)
    at_left = me_r < edge
    at_right = me_r >= n_rows - edge
    barrier = pltpu.get_barrier_semaphore()

    def greet(r, c):
        pl.semaphore_signal(barrier, inc=1, device_id=(r, c), device_id_type=MESH)

    def greet_near(d, carry):
        greet(lax.rem(me_r + d, n_rows), me_c)
        return carry

    lax.fori_loop(1, n_rows, greet_near, 0)

    def greet_side(to):
        def one(r, carry):
            greet(r, to)
            return carry

        lax.fori_loop(0, n_rows, one, 0)

    from_left = jnp.logical_and(at_left, has_left)
    from_right = jnp.logical_and(at_right, has_right)
    pl.when(from_left)(lambda: greet_side(left))
    pl.when(from_right)(lambda: greet_side(right))
    sides = jnp.minimum(me_c, 1) + jnp.minimum(n_cols - 1 - me_c, 1)
    pl.semaphore_wait(barrier, n_rows - 1 + edge * sides)

    def message(slot, side, r, c):
        return pltpu.make_async_remote_copy(
            src_ref=x_ref.at[slot],
            dst_ref=buf_ref.at[side, me_r],
            send_sem=send_sem.at[slot],
            recv_sem=recv_sem.at[side, me_r],
            device_id=(r, c),
            device_id_type=MESH,
        )

    def near(d, carry):
        r = lax.rem(me_r + d, n_rows)
        message(r, 0, r, me_c).start()
        return carry

    lax.fori_loop(1, n_rows, near, 0)

    @pl.when(has_left)
    def _():
        for e in range(edge):
            message(n_rows + e, 1, n_rows - edge + e, left).start()

    @pl.when(has_right)
    def _():
        for e in range(edge):
            message(n_rows + edge + e, 1, e, right).start()

    pltpu.make_async_copy(x_ref.at[me_r], buf_ref.at[0, me_r], recv_sem.at[0, me_r]).start()

    def wait_side(side):
        def one(r, carry):
            ref = buf_ref.at[side, r]
            pltpu.make_async_copy(ref, ref, recv_sem.at[side, r]).wait()
            return carry

        lax.fori_loop(0, n_rows, one, 0)

    wait_side(0)
    pl.when(from_left)(lambda: wait_side(1))
    pl.when(from_right)(lambda: wait_side(1))

    def sent(slot):
        pltpu.make_async_copy(x_ref.at[slot], x_ref.at[slot], send_sem.at[slot]).wait()

    def sent_near(d, carry):
        sent(lax.rem(me_r + d, n_rows))
        return carry

    lax.fori_loop(1, n_rows, sent_near, 0)

    @pl.when(has_left)
    def _():
        for e in range(edge):
            sent(n_rows + e)

    @pl.when(has_right)
    def _():
        for e in range(edge):
            sent(n_rows + edge + e)


def sweep(
    n_rows, n_cols, strip, halo, table_ref, count_ref, buf_ref, out_ref,
    vst, est, rst, gbuf, cost, pen, start, visits, splat, bad,
):
    total = cost.shape[0]
    width = n_rows * strip
    place = lax.axis_index("rows") * strip - halo
    begin = lax.axis_index("cols") * width + place
    lane = lax.broadcasted_iota(jnp.int32, (8, LANES), 1)
    col = lane + begin
    inside8 = jnp.logical_and(col >= 0, col < n_cols * width)
    here = jnp.logical_and(lane + place >= 0, lane + place < width)
    zero8 = jnp.zeros((8, LANES), jnp.float32)

    for g in range(2):
        for k in range(8):
            vst[g, k, 0:PAD, :] = zero8
            vst[g, k, PAD + total : PAD + total + PAD, :] = zero8
            gbuf[g, k, 0:PAD, :] = zero8
            gbuf[g, k, PAD + total : PAD + total + PAD, :] = zero8
    pen[0:PAD, :] = zero8
    pen[PAD + total : PAD + total + PAD, :] = zero8
    bad[...] = zero8
    for h in range(8):
        for k in range(8):
            splat[h * 8 + k] = jnp.full((8, LANES), count_ref[h, k], jnp.float32)
    for r in range(n_rows):
        rows = slice(r * 8, r * 8 + 8)

        def region(i):
            return jnp.where(inside8, jnp.where(here, buf_ref[0, r, i], buf_ref[1, r, i]), 0.0)

        cost[rows, :] = region(0)
        pen[PAD + r * 8 : PAD + r * 8 + 8, :] = region(1)
        start[rows, :] = region(2)

    inside = jnp.broadcast_to(inside8[None], (CHUNK // 8, 8, LANES)).reshape(CHUNK, LANES)
    chunks = [c * CHUNK for c in range(total // CHUNK)]

    def run(direct):
        for k in range(8):
            for r0 in chunks:
                vst[0, k, PAD + r0 : PAD + r0 + CHUNK, :] = jnp.zeros((CHUNK, LANES), jnp.float32)

        def back_step(n, carry):
            now = lax.rem(n, 2)
            for r0 in chunks:
                rows = slice(r0, r0 + CHUNK)
                shifted = []
                for k in range(8):
                    at = slice(PAD + r0 + ROW_STEP[k], PAD + r0 + ROW_STEP[k] + CHUNK)
                    value = vst[now, k, at, :] + pen[at, :]
                    if COL_STEP[k]:
                        value = pltpu.roll(value, (-COL_STEP[k]) % LANES, 1)
                    shifted.append(value)
                if not direct:
                    largest = functools.reduce(jnp.maximum, shifted)
                    for k in range(8):
                        est[n, k, rows, :] = jnp.exp2(shifted[k] - largest)
                else:
                    for k in range(8):
                        est[n, k, rows, :] = shifted[k]
                smallest = None
                for h in range(8):
                    chosen = [est[n, table_ref[h, a], rows, :] for a in range(8)]
                    if direct:
                        largest = functools.reduce(jnp.maximum, chosen)
                        chosen = [jnp.exp2(q - largest) for q in chosen]
                    while len(chosen) > 1:
                        chosen = [chosen[i] + chosen[i + 1] for i in range(0, len(chosen), 2)]
                    sums = chosen[0]
                    level = jnp.log2(sums) + largest
                    rst[n, h, rows, :] = level if direct else 1.0 / sums
                    vst[1 - now, h, PAD + r0 : PAD + r0 + CHUNK, :] = jnp.where(
                        inside, level - cost[rows, :], 0.0
                    )
                    smallest = sums if h == 0 else jnp.minimum(smallest, sums)
                if not direct:
                    for i in range(CHUNK // 8):
                        ok = smallest[i * 8 : i * 8 + 8] >= SMALLEST
                        bad[...] = jnp.where(ok, bad[...], 1.0)
            return carry

        lax.fori_loop(0, ITERS, back_step, 0)

        def flow(n, slot, r0, density):
            rows = slice(r0, r0 + CHUNK)
            at = slice(PAD + r0, PAD + r0 + CHUNK)

            def weight(h, k):
                one = splat[h * 8 + k]
                return jnp.broadcast_to(one[None], (CHUNK // 8, 8, LANES)).reshape(CHUNK, LANES)

            if not direct:
                scaled = [density[h] * rst[n, h, rows, :] for h in range(8)]
                for k in range(8):
                    mass = functools.reduce(
                        jnp.add, [weight(h, k) * scaled[h] for h in range(8)]
                    )
                    gbuf[slot, k, at, :] = mass * est[n, k, rows, :]
            else:
                for k in range(8):
                    here = est[n, k, rows, :]
                    mass = jnp.zeros((CHUNK, LANES), jnp.float32)
                    for h in range(8):
                        policy = jnp.exp2(jnp.minimum(here - rst[n, h, rows, :], 0.0))
                        mass = mass + weight(h, k) * (density[h] * policy)
                    gbuf[slot, k, at, :] = mass

        def arrive(slot, r0):
            density = []
            for k in range(8):
                at = slice(PAD + r0 - ROW_STEP[k], PAD + r0 - ROW_STEP[k] + CHUNK)
                mass = gbuf[slot, k, at, :]
                if COL_STEP[k]:
                    mass = pltpu.roll(mass, COL_STEP[k] % LANES, 1)
                density.append(jnp.where(inside, mass, 0.0))
            return density

        for r0 in chunks:
            first = start[r0 : r0 + CHUNK, :]
            flow(ITERS - 1, 0, r0, [first] * 8)
            visits[r0 : r0 + CHUNK, :] = jnp.zeros((CHUNK, LANES), jnp.float32)

        def forward_step(t, carry):
            slot = lax.rem(t + 1, 2)
            for r0 in chunks:
                rows = slice(r0, r0 + CHUNK)
                density = arrive(slot, r0)
                visits[rows, :] = visits[rows, :] + functools.reduce(jnp.add, density)
                flow(ITERS - 1 - t, 1 - slot, r0, density)
            return carry

        lax.fori_loop(1, ITERS, forward_step, 0)
        for r0 in chunks:
            rows = slice(r0, r0 + CHUNK)
            density = arrive((ITERS - 1) % 2, r0)
            visits[rows, :] = visits[rows, :] + functools.reduce(jnp.add, density)

    run(False)
    pl.when(jnp.max(bad[...]) > 0.0)(lambda: run(True))

    group = LANES // strip
    packs = out_ref.shape[1] - 1
    scale = 1.0 / (LOG2E * ITERS)
    for r in range(n_rows):
        at = slice(PAD + r * 8, PAD + r * 8 + 8)
        for p in range(packs):
            packed = zero8
            for g in range(min(group, 8)):
                value = pltpu.roll(vst[ITERS % 2, p * group + g, at, :], (g * strip - halo) % LANES, 1)
                low = g * strip
                keep = jnp.logical_and(lane >= low, lane < low + strip)
                packed = jnp.where(keep, value, packed)
            out_ref[r, p] = packed * scale
        out_ref[r, packs] = pltpu.roll(visits[r * 8 : r * 8 + 8, :], (-halo) % LANES, 1)


def scatter(n_rows, strip, x_ref, values_ref, visits_ref, recv, send_sem, recv_sem):
    me_r = lax.axis_index("rows")
    me_c = lax.axis_index("cols")
    barrier = pltpu.get_barrier_semaphore()

    def greet(d, carry):
        to = lax.rem(me_r + d, n_rows)
        pl.semaphore_signal(barrier, inc=1, device_id=(to, me_c), device_id_type=MESH)
        return carry

    lax.fori_loop(1, n_rows, greet, 0)
    pl.semaphore_wait(barrier, n_rows - 1)
    local = pltpu.make_async_copy(x_ref.at[me_r], recv.at[me_r], recv_sem.at[me_r])
    local.start()

    def partner(d):
        return lax.rem(me_r + d, n_rows)

    def send(d, carry):
        to = partner(d)
        pltpu.make_async_remote_copy(
            src_ref=x_ref.at[to],
            dst_ref=recv.at[me_r],
            send_sem=send_sem.at[to],
            recv_sem=recv_sem.at[me_r],
            device_id=(to, me_c),
            device_id_type=MESH,
        ).start()
        return carry

    lax.fori_loop(1, n_rows, send, 0)

    def arrived(r, carry):
        pltpu.make_async_copy(recv.at[r], recv.at[r], recv_sem.at[r]).wait()
        return carry

    lax.fori_loop(0, n_rows, arrived, 0)
    group = LANES // strip
    packs = x_ref.shape[1] - 1
    lane = lax.broadcasted_iota(jnp.int32, (8, LANES), 1)
    width = visits_ref.shape[-1]
    for q in range(width // LANES):
        cols = slice(q * LANES, (q + 1) * LANES)

        def assemble(pack, source):
            whole = None
            for i in range(group):
                piece = recv[q * group + i, pack]
                move = (i * strip - source) % LANES
                if move:
                    piece = pltpu.roll(piece, move, 1)
                whole = piece if i == 0 else jnp.where(lane >= i * strip, piece, whole)
            return whole

        for h in range(8):
            values_ref[h, :, cols] = assemble(h // group, (h % group) * strip)
        visits_ref[:, cols] = assemble(packs, 0)

    def sent(d, carry):
        to = partner(d)
        pltpu.make_async_copy(x_ref.at[to], x_ref.at[to], send_sem.at[to]).wait()
        return carry

    lax.fori_loop(1, n_rows, sent, 0)


def on_device(n_rows, n_cols, cell_cost, blocked, move_table, anchor_cells, anchor_mass):
    height, width = cell_cost.shape
    strip = width // n_rows
    halo = (LANES - strip) // 2
    assert height == 8 and strip * n_rows == width and halo >= 2 * ITERS
    total = height * n_rows
    group = LANES // strip
    packs = -(-8 // group)
    vmem = pl.BlockSpec(memory_space=pltpu.VMEM)
    smem = pl.BlockSpec(memory_space=pltpu.SMEM)
    f32 = jnp.float32

    edge = -(-halo // strip)

    tile, counts = pl.pallas_call(
        functools.partial(prepare, n_rows, strip, halo),
        out_shape=(
            jax.ShapeDtypeStruct((n_rows + 2 * edge, 3, height, LANES), f32),
            jax.ShapeDtypeStruct((8, 8), f32),
        ),
        in_specs=[vmem] * 5,
        out_specs=(vmem, vmem),
        name="prepare",
    )(cell_cost, blocked, move_table, anchor_cells, anchor_mass)

    buf = pl.pallas_call(
        functools.partial(gather, n_rows, n_cols, edge),
        out_shape=jax.ShapeDtypeStruct((2, n_rows, 3, height, LANES), f32),
        in_specs=[vmem],
        out_specs=vmem,
        scratch_shapes=[
            pltpu.SemaphoreType.DMA((n_rows + 2 * edge,)),
            pltpu.SemaphoreType.DMA((2, n_rows)),
        ],
        compiler_params=pltpu.CompilerParams(collective_id=0, has_side_effects=True),
        name="gather",
    )(tile)

    padded = total + 2 * PAD
    packed = pl.pallas_call(
        functools.partial(sweep, n_rows, n_cols, strip, halo),
        out_shape=jax.ShapeDtypeStruct((n_rows, packs + 1, height, LANES), f32),
        in_specs=[smem, smem, vmem],
        out_specs=vmem,
        scratch_shapes=[
            pltpu.VMEM((2, 8, padded, LANES), f32),
            pltpu.VMEM((ITERS, 8, total, LANES), f32),
            pltpu.VMEM((ITERS, 8, total, LANES), f32),
            pltpu.VMEM((2, 8, padded, LANES), f32),
            pltpu.VMEM((total, LANES), f32),
            pltpu.VMEM((padded, LANES), f32),
            pltpu.VMEM((total, LANES), f32),
            pltpu.VMEM((total, LANES), f32),
            pltpu.VMEM((64, 8, LANES), f32),
            pltpu.VMEM((8, LANES), f32),
        ],
        compiler_params=pltpu.CompilerParams(vmem_limit_bytes=67043328),
        name="sweep",
    )(move_table, counts, buf)

    return pl.pallas_call(
        functools.partial(scatter, n_rows, strip),
        out_shape=(
            jax.ShapeDtypeStruct((8, height, width), f32),
            jax.ShapeDtypeStruct((height, width), f32),
        ),
        in_specs=[vmem],
        out_specs=(vmem, vmem),
        scratch_shapes=[
            pltpu.VMEM((n_rows, packs + 1, height, LANES), f32),
            pltpu.SemaphoreType.DMA((n_rows,)),
            pltpu.SemaphoreType.DMA((n_rows,)),
        ],
        compiler_params=pltpu.CompilerParams(collective_id=1, has_side_effects=True),
        name="scatter",
    )(packed)


def solution(mesh):
    placed = (
        P("rows", "cols"),
        P("rows", "cols"),
        P(),
        P("rows", "cols", None),
        P("rows", "cols", None),
    )
    return jax.shard_map(
        functools.partial(on_device, mesh.shape["rows"], mesh.shape["cols"]),
        mesh=mesh,
        in_specs=placed,
        out_specs=(P(None, "rows", "cols"), P("rows", "cols")),
        check_vma=False,
    )
```

```python
import functools
import math

import jax
import jax.numpy as jnp
from jax import lax
from jax.experimental import pallas as pl
from jax.experimental.pallas import tpu as pltpu
from jax.sharding import PartitionSpec as P

ITERS = 20
PENALTY = 3.0
ROW_STEP = (0, -1, -1, -1, 0, 1, 1, 1)
COL_STEP = (1, 1, 0, -1, -1, -1, 0, 1)
MESH = pl.DeviceIdType.MESH
LANES = 128
LOG2E = math.log2(math.e)
SMALLEST = 2.0**-60
CHUNK = 32
PAD = 8


def prepare(n_rows, strip, halo, cost_ref, blocked_ref, table_ref, cells_ref, mass_ref, out_ref, count_ref):
    height, width = cost_ref.shape
    entries = cells_ref.shape[-1]
    cells = cells_ref[...].reshape(1, entries)
    masses = mass_ref[...].reshape(1, entries) * 0.125
    row = jnp.zeros((1, entries), jnp.int32)
    for i in range(1, height):
        row = row + (cells >= i * width).astype(jnp.int32)
    col = cells - row * width
    rows = lax.broadcasted_iota(jnp.int32, (height, entries), 0)
    cols = lax.broadcasted_iota(jnp.int32, (width, entries), 0)
    at_row = jnp.where(rows == row, masses, 0.0)
    at_col = (cols == col).astype(jnp.float32)
    start = lax.dot_general(
        at_row,
        at_col,
        (((1,), (1,)), ((), ())),
        precision=lax.Precision.HIGHEST,
        preferred_element_type=jnp.float32,
    )
    fields = (
        cost_ref[...] * LOG2E,
        blocked_ref[...].astype(jnp.float32) * (-PENALTY * LOG2E),
        start,
    )
    lane = lax.broadcasted_iota(jnp.int32, (height, LANES), 1)
    zero = jnp.zeros((height, LANES), jnp.float32)
    edge = -(-halo // strip)
    for slot, place in enumerate([*range(n_rows), *range(-edge, 0), *range(n_rows, n_rows + edge)]):
        begin = place * strip - halo
        block, off = begin // LANES, begin % LANES
        for f, field in enumerate(fields):

            def part(b):
                if b < 0 or b >= width // LANES:
                    return zero
                piece = field[:, b * LANES : (b + 1) * LANES]
                return pltpu.roll(piece, LANES - off, 1) if off else piece

            out_ref[slot, f] = jnp.where(lane < LANES - off, part(block), part(block + 1))

    table = table_ref[...]
    heading = lax.broadcasted_iota(jnp.int32, table.shape, 1)
    counts = jnp.zeros(table.shape, jnp.float32)
    for k in range(8):
        times = jnp.sum((table == k).astype(jnp.float32), axis=1, keepdims=True)
        counts = jnp.where(heading == k, times, counts)
    count_ref[...] = counts


def gather(n_rows, n_cols, edge, x_ref, buf_ref, send_sem, recv_sem):
    me_r = lax.axis_index("rows")
    me_c = lax.axis_index("cols")
    has_left = me_c > 0
    has_right = me_c < n_cols - 1
    left = jnp.maximum(me_c - 1, 0)
    right = jnp.minimum(me_c + 1, n_cols - 1)
    at_left = me_r < edge
    at_right = me_r >= n_rows - edge
    barrier = pltpu.get_barrier_semaphore()

    def greet(r, c):
        pl.semaphore_signal(barrier, inc=1, device_id=(r, c), device_id_type=MESH)

    def greet_near(d, carry):
        greet(lax.rem(me_r + d, n_rows), me_c)
        return carry

    lax.fori_loop(1, n_rows, greet_near, 0)

    def greet_side(to):
        def one(r, carry):
            greet(r, to)
            return carry

        lax.fori_loop(0, n_rows, one, 0)

    from_left = jnp.logical_and(at_left, has_left)
    from_right = jnp.logical_and(at_right, has_right)
    pl.when(from_left)(lambda: greet_side(left))
    pl.when(from_right)(lambda: greet_side(right))
    sides = jnp.minimum(me_c, 1) + jnp.minimum(n_cols - 1 - me_c, 1)
    pl.semaphore_wait(barrier, n_rows - 1 + edge * sides)

    def message(slot, side, r, c):
        return pltpu.make_async_remote_copy(
            src_ref=x_ref.at[slot],
            dst_ref=buf_ref.at[side, me_r],
            send_sem=send_sem.at[slot],
            recv_sem=recv_sem.at[side, me_r],
            device_id=(r, c),
            device_id_type=MESH,
        )

    def near(d, carry):
        r = lax.rem(me_r + d, n_rows)
        message(r, 0, r, me_c).start()
        return carry

    lax.fori_loop(1, n_rows, near, 0)

    @pl.when(has_left)
    def _():
        for e in range(edge):
            message(n_rows + e, 1, n_rows - edge + e, left).start()

    @pl.when(has_right)
    def _():
        for e in range(edge):
            message(n_rows + edge + e, 1, e, right).start()

    pltpu.make_async_copy(x_ref.at[me_r], buf_ref.at[0, me_r], recv_sem.at[0, me_r]).start()

    def wait_side(side):
        def one(r, carry):
            ref = buf_ref.at[side, r]
            pltpu.make_async_copy(ref, ref, recv_sem.at[side, r]).wait()
            return carry

        lax.fori_loop(0, n_rows, one, 0)

    wait_side(0)
    pl.when(from_left)(lambda: wait_side(1))
    pl.when(from_right)(lambda: wait_side(1))

    def sent(slot):
        pltpu.make_async_copy(x_ref.at[slot], x_ref.at[slot], send_sem.at[slot]).wait()

    def sent_near(d, carry):
        sent(lax.rem(me_r + d, n_rows))
        return carry

    lax.fori_loop(1, n_rows, sent_near, 0)

    @pl.when(has_left)
    def _():
        for e in range(edge):
            sent(n_rows + e)

    @pl.when(has_right)
    def _():
        for e in range(edge):
            sent(n_rows + edge + e)


def sweep(
    n_rows, n_cols, strip, halo, table_ref, count_ref, buf_ref, out_ref,
    vst, est, rst, gbuf, cost, pen, start, visits, splat, bad,
):
    total = cost.shape[0]
    width = n_rows * strip
    place = lax.axis_index("rows") * strip - halo
    begin = lax.axis_index("cols") * width + place
    lane = lax.broadcasted_iota(jnp.int32, (8, LANES), 1)
    col = lane + begin
    inside8 = jnp.logical_and(col >= 0, col < n_cols * width)
    here = jnp.logical_and(lane + place >= 0, lane + place < width)
    zero8 = jnp.zeros((8, LANES), jnp.float32)

    for g in range(2):
        for k in range(8):
            vst[g, k, 0:PAD, :] = zero8
            vst[g, k, PAD + total : PAD + total + PAD, :] = zero8
            gbuf[g, k, 0:PAD, :] = zero8
            gbuf[g, k, PAD + total : PAD + total + PAD, :] = zero8
    pen[0:PAD, :] = zero8
    pen[PAD + total : PAD + total + PAD, :] = zero8
    bad[...] = zero8
    for h in range(8):
        for k in range(8):
            splat[h * 8 + k] = jnp.full((8, LANES), count_ref[h, k], jnp.float32)
    for r in range(n_rows):
        rows = slice(r * 8, r * 8 + 8)

        def region(i):
            return jnp.where(inside8, jnp.where(here, buf_ref[0, r, i], buf_ref[1, r, i]), 0.0)

        cost[rows, :] = region(0)
        pen[PAD + r * 8 : PAD + r * 8 + 8, :] = region(1)
        start[rows, :] = region(2)

    inside = jnp.broadcast_to(inside8[None], (CHUNK // 8, 8, LANES)).reshape(CHUNK, LANES)
    chunks = [c * CHUNK for c in range(total // CHUNK)]

    def run(direct):
        for k in range(8):
            for r0 in chunks:
                vst[0, k, PAD + r0 : PAD + r0 + CHUNK, :] = jnp.zeros((CHUNK, LANES), jnp.float32)

        def weight(h, k):
            one = splat[h * 8 + k]
            return jnp.broadcast_to(one[None], (CHUNK // 8, 8, LANES)).reshape(CHUNK, LANES)

        def back_step(n, carry):
            now = lax.rem(n, 2)
            for r0 in chunks:
                rows = slice(r0, r0 + CHUNK)
                shifted = []
                for k in range(8):
                    at = slice(PAD + r0 + ROW_STEP[k], PAD + r0 + ROW_STEP[k] + CHUNK)
                    value = vst[now, k, at, :] + pen[at, :]
                    if COL_STEP[k]:
                        value = pltpu.roll(value, (-COL_STEP[k]) % LANES, 1)
                    shifted.append(value)
                if not direct:
                    largest = functools.reduce(jnp.maximum, shifted)
                    ratios = [jnp.exp2(shifted[k] - largest) for k in range(8)]
                    for k in range(8):
                        est[n, k, rows, :] = ratios[k]
                else:
                    for k in range(8):
                        est[n, k, rows, :] = shifted[k]
                smallest = None
                for h in range(8):
                    if direct:
                        chosen = [est[n, table_ref[h, a], rows, :] for a in range(8)]
                    else:
                        chosen = [weight(h, k) * ratios[k] for k in range(8)]
                    if direct:
                        largest = functools.reduce(jnp.maximum, chosen)
                        chosen = [jnp.exp2(q - largest) for q in chosen]
                    while len(chosen) > 1:
                        chosen = [chosen[i] + chosen[i + 1] for i in range(0, len(chosen), 2)]
                    sums = chosen[0]
                    level = jnp.log2(sums) + largest
                    rst[n, h, rows, :] = level if direct else 1.0 / sums
                    vst[1 - now, h, PAD + r0 : PAD + r0 + CHUNK, :] = jnp.where(
                        inside, level - cost[rows, :], 0.0
                    )
                    smallest = sums if h == 0 else jnp.minimum(smallest, sums)
                if not direct:
                    for i in range(CHUNK // 8):
                        ok = smallest[i * 8 : i * 8 + 8] >= SMALLEST
                        bad[...] = jnp.where(ok, bad[...], 1.0)
            return carry

        lax.fori_loop(0, ITERS, back_step, 0)

        def flow(n, slot, r0, density):
            rows = slice(r0, r0 + CHUNK)
            at = slice(PAD + r0, PAD + r0 + CHUNK)

            if not direct:
                scaled = [density[h] * rst[n, h, rows, :] for h in range(8)]
                for k in range(8):
                    mass = functools.reduce(
                        jnp.add, [weight(h, k) * scaled[h] for h in range(8)]
                    )
                    gbuf[slot, k, at, :] = mass * est[n, k, rows, :]
            else:
                for k in range(8):
                    here = est[n, k, rows, :]
                    mass = jnp.zeros((CHUNK, LANES), jnp.float32)
                    for h in range(8):
                        policy = jnp.exp2(jnp.minimum(here - rst[n, h, rows, :], 0.0))
                        mass = mass + weight(h, k) * (density[h] * policy)
                    gbuf[slot, k, at, :] = mass

        def arrive(slot, r0):
            density = []
            for k in range(8):
                at = slice(PAD + r0 - ROW_STEP[k], PAD + r0 - ROW_STEP[k] + CHUNK)
                mass = gbuf[slot, k, at, :]
                if COL_STEP[k]:
                    mass = pltpu.roll(mass, COL_STEP[k] % LANES, 1)
                density.append(jnp.where(inside, mass, 0.0))
            return density

        for r0 in chunks:
            first = start[r0 : r0 + CHUNK, :]
            flow(ITERS - 1, 0, r0, [first] * 8)
            visits[r0 : r0 + CHUNK, :] = jnp.zeros((CHUNK, LANES), jnp.float32)

        def forward_step(t, carry):
            slot = lax.rem(t + 1, 2)
            for r0 in chunks:
                rows = slice(r0, r0 + CHUNK)
                density = arrive(slot, r0)
                visits[rows, :] = visits[rows, :] + functools.reduce(jnp.add, density)
                flow(ITERS - 1 - t, 1 - slot, r0, density)
            return carry

        lax.fori_loop(1, ITERS, forward_step, 0)
        for r0 in chunks:
            rows = slice(r0, r0 + CHUNK)
            density = arrive((ITERS - 1) % 2, r0)
            visits[rows, :] = visits[rows, :] + functools.reduce(jnp.add, density)

    run(False)
    pl.when(jnp.max(bad[...]) > 0.0)(lambda: run(True))

    group = LANES // strip
    packs = out_ref.shape[1] - 1
    scale = 1.0 / (LOG2E * ITERS)
    for r in range(n_rows):
        at = slice(PAD + r * 8, PAD + r * 8 + 8)
        for p in range(packs):
            packed = zero8
            for g in range(min(group, 8)):
                value = pltpu.roll(vst[ITERS % 2, p * group + g, at, :], (g * strip - halo) % LANES, 1)
                low = g * strip
                keep = jnp.logical_and(lane >= low, lane < low + strip)
                packed = jnp.where(keep, value, packed)
            out_ref[r, p] = packed * scale
        out_ref[r, packs] = pltpu.roll(visits[r * 8 : r * 8 + 8, :], (-halo) % LANES, 1)


def scatter(n_rows, x_ref, recv, send_sem, recv_sem):
    me_r = lax.axis_index("rows")
    me_c = lax.axis_index("cols")
    barrier = pltpu.get_barrier_semaphore()

    def greet(d, carry):
        to = lax.rem(me_r + d, n_rows)
        pl.semaphore_signal(barrier, inc=1, device_id=(to, me_c), device_id_type=MESH)
        return carry

    lax.fori_loop(1, n_rows, greet, 0)
    pl.semaphore_wait(barrier, n_rows - 1)
    local = pltpu.make_async_copy(x_ref.at[me_r], recv.at[me_r], recv_sem.at[me_r])
    local.start()

    def partner(d):
        return lax.rem(me_r + d, n_rows)

    def send(d, carry):
        to = partner(d)
        pltpu.make_async_remote_copy(
            src_ref=x_ref.at[to],
            dst_ref=recv.at[me_r],
            send_sem=send_sem.at[to],
            recv_sem=recv_sem.at[me_r],
            device_id=(to, me_c),
            device_id_type=MESH,
        ).start()
        return carry

    lax.fori_loop(1, n_rows, send, 0)

    def arrived(r, carry):
        pltpu.make_async_copy(recv.at[r], recv.at[r], recv_sem.at[r]).wait()
        return carry

    lax.fori_loop(0, n_rows, arrived, 0)
    def sent(d, carry):
        to = partner(d)
        pltpu.make_async_copy(x_ref.at[to], x_ref.at[to], send_sem.at[to]).wait()
        return carry

    lax.fori_loop(1, n_rows, sent, 0)


def unpack(strip, recv, values_ref, visits_ref):
    group = LANES // strip
    packs = recv.shape[1] - 1
    lane = lax.broadcasted_iota(jnp.int32, (8, LANES), 1)
    width = visits_ref.shape[-1]
    for q in range(width // LANES):
        cols = slice(q * LANES, (q + 1) * LANES)

        def assemble(pack, source):
            whole = None
            for i in range(group):
                piece = recv[q * group + i, pack]
                move = (i * strip - source) % LANES
                if move:
                    piece = pltpu.roll(piece, move, 1)
                whole = piece if i == 0 else jnp.where(lane >= i * strip, piece, whole)
            return whole

        for h in range(8):
            values_ref[h, :, cols] = assemble(h // group, (h % group) * strip)
        visits_ref[:, cols] = assemble(packs, 0)


def on_device(n_rows, n_cols, cell_cost, blocked, move_table, anchor_cells, anchor_mass):
    height, width = cell_cost.shape
    strip = width // n_rows
    halo = (LANES - strip) // 2
    assert height == 8 and strip * n_rows == width and halo >= 2 * ITERS
    total = height * n_rows
    group = LANES // strip
    packs = -(-8 // group)
    vmem = pl.BlockSpec(memory_space=pltpu.VMEM)
    smem = pl.BlockSpec(memory_space=pltpu.SMEM)
    f32 = jnp.float32

    edge = -(-halo // strip)

    tile, counts = pl.pallas_call(
        functools.partial(prepare, n_rows, strip, halo),
        out_shape=(
            jax.ShapeDtypeStruct((n_rows + 2 * edge, 3, height, LANES), f32),
            jax.ShapeDtypeStruct((8, 8), f32),
        ),
        in_specs=[vmem] * 5,
        out_specs=(vmem, vmem),
        name="prepare",
    )(cell_cost, blocked, move_table, anchor_cells, anchor_mass)

    buf = pl.pallas_call(
        functools.partial(gather, n_rows, n_cols, edge),
        out_shape=jax.ShapeDtypeStruct((2, n_rows, 3, height, LANES), f32),
        in_specs=[vmem],
        out_specs=vmem,
        scratch_shapes=[
            pltpu.SemaphoreType.DMA((n_rows + 2 * edge,)),
            pltpu.SemaphoreType.DMA((2, n_rows)),
        ],
        compiler_params=pltpu.CompilerParams(collective_id=0, has_side_effects=True),
        name="gather",
    )(tile)

    padded = total + 2 * PAD
    packed = pl.pallas_call(
        functools.partial(sweep, n_rows, n_cols, strip, halo),
        out_shape=jax.ShapeDtypeStruct((n_rows, packs + 1, height, LANES), f32),
        in_specs=[smem, smem, vmem],
        out_specs=vmem,
        scratch_shapes=[
            pltpu.VMEM((2, 8, padded, LANES), f32),
            pltpu.VMEM((ITERS, 8, total, LANES), f32),
            pltpu.VMEM((ITERS, 8, total, LANES), f32),
            pltpu.VMEM((2, 8, padded, LANES), f32),
            pltpu.VMEM((total, LANES), f32),
            pltpu.VMEM((padded, LANES), f32),
            pltpu.VMEM((total, LANES), f32),
            pltpu.VMEM((total, LANES), f32),
            pltpu.VMEM((64, 8, LANES), f32),
            pltpu.VMEM((8, LANES), f32),
        ],
        compiler_params=pltpu.CompilerParams(vmem_limit_bytes=67043328),
        name="sweep",
    )(move_table, counts, buf)

    received = pl.pallas_call(
        functools.partial(scatter, n_rows),
        out_shape=jax.ShapeDtypeStruct(packed.shape, f32),
        in_specs=[vmem],
        out_specs=vmem,
        scratch_shapes=[
            pltpu.SemaphoreType.DMA((n_rows,)),
            pltpu.SemaphoreType.DMA((n_rows,)),
        ],
        compiler_params=pltpu.CompilerParams(collective_id=1, has_side_effects=True),
        name="scatter",
    )(packed)

    return pl.pallas_call(
        functools.partial(unpack, strip),
        out_shape=(
            jax.ShapeDtypeStruct((8, height, width), f32),
            jax.ShapeDtypeStruct((height, width), f32),
        ),
        in_specs=[vmem],
        out_specs=(vmem, vmem),
        name="unpack",
    )(received)


def solution(mesh):
    placed = (
        P("rows", "cols"),
        P("rows", "cols"),
        P(),
        P("rows", "cols", None),
        P("rows", "cols", None),
    )
    return jax.shard_map(
        functools.partial(on_device, mesh.shape["rows"], mesh.shape["cols"]),
        mesh=mesh,
        in_specs=placed,
        out_specs=(P(None, "rows", "cols"), P("rows", "cols")),
        check_vma=False,
    )
```
